32 devices in a mesh: gy: 8 (over y, x, core), gz: 4 (over z).
Axes of the slice: x: 2, y: 2, z: 4, core: 2. Of those that a mesh axis runs over, the one named last changes fastest.
Arguments:
- fuel: float32 [128, 16, 2048], P('gy', 'gz'), may hold values from -6 to 6
- oxidant: float32 [128, 16, 2048], P('gy', 'gz'), may hold values from -6 to 6
- rate: float32 [128, 16, 2048], P('gy', 'gz'), may hold values from 0.05 to 0.5
- velocity: float32 [3], replicated, may hold values from -0.3 to 0.3
- sketch_x: float32 [128, 2048], replicated, may hold values from -0.125 to 0.125
- sketch_y: float32 [128, 128], replicated, may hold values from -0.5 to 0.5
Outputs:
- sketch: float32 [128, 2, 16, 128], P('gy', None, 'gz')
The draws below stay inside these ranges and needn't reach their ends.
All inputs are finite; a program needn't handle non-finite values.
Results may differ from the reference program's by a relative error of at most 0.00014.
Values sent between devices are 32-bit elements; how exact they have to be, the bound alone decides.
No kernel may reach another device: no remote copies, remote signals or barrier semaphores. Data moves between devices by JAX's collectives and lax.ppermute only.
A program may use at most 64 MiB of HBM per device.

```python
import math
import jax
import jax.numpy as jnp
from jax import lax

X = 2048
K = 128
STEPS = 2
NY = 128
NZ = 16


def block_levels(rng, extent, pieces, least, high):
    loudness, own = 1.0, jax.random.fold_in(rng, 6)
    for dim, parts in pieces:
        steps = jnp.exp(jax.random.uniform(jax.random.fold_in(own, dim), (parts,), jnp.float32, least / len(pieces), high / len(pieces)))
        loudness = loudness * jnp.repeat(steps, extent[dim] // parts).reshape([-1 if axis == dim else 1 for axis in range(len(extent))])
    return loudness


def bell_draw(rng, dims, spread, reach, split=(), kind=jnp.bfloat16):
    loudness = block_levels(rng, dims, split, -0.22, 0.18) if split else 1.0
    array = jax.random.normal(rng, dims, jnp.float32) * spread * loudness
    return jnp.minimum(jnp.maximum(array, -reach), reach).astype(kind)


def setup_inputs(seed: int = 0) -> dict:
    splits = jax.random.split(jax.random.key(seed), 7)
    fuel = bell_draw(splits[0], (NY, NZ, X), 1.0, 6.0, ((0, 8), (1, 4)), jnp.float32)
    oxidant = bell_draw(splits[1], (NY, NZ, X), 1.0, 6.0, ((0, 8), (1, 4)), jnp.float32)
    rate = jnp.clip(jnp.exp(math.log(0.5) - 2.3025851 * jax.random.uniform(splits[2], (NY, NZ, X), jnp.float32) ** block_levels(splits[2], (NY, NZ, X), ((0, 8), (1, 4)), -0.2, 0.2)), 0.05, 0.5)
    velocity = jnp.clip(jax.random.uniform(splits[3], (3,), jnp.float32, -0.3, 0.3), -0.3, 0.3)
    sketch_x = bell_draw(splits[4], (K, X), X ** -0.5, 0.125, (), jnp.float32)
    sketch_y = bell_draw(splits[5], (K, NY), NY ** -0.5, 0.5, (), jnp.float32)
    return {"fuel": fuel, "oxidant": oxidant, "rate": rate, "velocity": velocity, "sketch_x": sketch_x, "sketch_y": sketch_y}


def advance(padded, rate, velocity):
    core = padded[:, 1:-1, 1:-1, :]
    xpad = jnp.pad(core, ((0, 0), (0, 0), (0, 0), (1, 1)))
    east = xpad[..., 2:]
    west = xpad[..., :-2]
    north = padded[:, 2:, 1:-1, :]
    south = padded[:, :-2, 1:-1, :]
    upper = padded[:, 1:-1, 2:, :]
    lower = padded[:, 1:-1, :-2, :]
    lap = east + west + north + south + upper + lower - 6.0 * core
    adv = 0.5 * (velocity[0] * (east - west) + velocity[1] * (north - south) + velocity[2] * (upper - lower))
    react = rate * core[0] * core[1]
    new_fuel = core[0] + 0.1 * lap[0] - adv[0] - react
    new_oxid = core[1] + 0.05 * lap[1] - adv[1] + react
    return jnp.stack([new_fuel, new_oxid])


def reference(fuel, oxidant, rate, velocity, sketch_x, sketch_y):
    fields = jnp.stack([fuel, oxidant])
    for step in range(STEPS):
        padded = jnp.pad(fields, ((0, 0), (1, 1), (1, 1), (0, 0)))
        fields = advance(padded, rate, velocity)
    projected = jnp.einsum("kx,fyzx->kfyz", sketch_x, fields, precision=lax.Precision.HIGHEST)
    return jnp.einsum("kfyz,jy->kfzj", projected, sketch_y, precision=lax.Precision.HIGHEST)
```

```python
import functools

import jax
import jax.numpy as jnp
from jax import lax
from jax.experimental import pallas as pl
from jax.experimental.pallas import tpu as pltpu
from jax.sharding import PartitionSpec as P

DIFFUSION = (0.1, 0.05)
F32 = jnp.float32
BF16 = jnp.bfloat16
LANES = 128
VMEM_LIMIT = 16 * 1024 * 1024


def swaps(count, first):
    out = []
    for i in range(first, count - 1, 2):
        out += [(i, i + 1), (i + 1, i)]
    return out


def lane_view(cells):
    rows, planes, width = cells.shape
    tiles = width // LANES
    return (
        cells.reshape(rows, planes, tiles, LANES)
        .transpose(0, 2, 1, 3)
        .reshape(rows * tiles * planes, LANES)
    )


def call(body, outs, n_in, smem=(), aliases=None, scratch=(), flops=0, size=0):
    specs = [
        pl.BlockSpec(memory_space=pltpu.SMEM if i in smem else pltpu.VMEM)
        for i in range(n_in)
    ]
    return pl.pallas_call(
        body,
        out_shape=[jax.ShapeDtypeStruct(s, d) for s, d in outs],
        in_specs=specs,
        out_specs=[pl.BlockSpec(memory_space=pltpu.VMEM) for _ in outs],
        scratch_shapes=scratch,
        input_output_aliases=aliases or {},
        compiler_params=pltpu.CompilerParams(vmem_limit_bytes=VMEM_LIMIT),
        cost_estimate=pl.CostEstimate(flops=flops, bytes_accessed=size, transcendentals=0),
    )


def split(x):
    high = x.astype(BF16)
    return high, (x - high.astype(F32)).astype(BF16)


def product(a, b):
    return lax.dot_general(a, b, (((1,), (1,)), ((), ())), preferred_element_type=F32)


def project(x, s_high, s_low):
    high, low = split(x)
    return product(high, s_high) + product(low, s_high) + product(high, s_low)


def along_x(c, d, v):
    width = c.shape[1]
    lane = lax.broadcasted_iota(jnp.int32, c.shape, 1)
    east = jnp.where(lane == width - 1, 0.0, pltpu.roll(c, width - 1, 1))
    west = jnp.where(lane == 0, 0.0, pltpu.roll(c, 1, 1))
    return (1.0 - 6.0 * d) * c + (d - 0.5 * v) * east + (d + 0.5 * v) * west


def edge_planes(planes):
    odd = lax.rem(lax.axis_index("gz"), 2)
    first = jnp.where(odd == 0, planes - 1, 0)
    return first, planes - 1 - first


def faces_kernel(dims, a_ref, b_ref, za_ref, zb_ref, ya_ref, yb_ref):
    rows, planes, width = dims
    tiles = width // LANES
    pa, pb = edge_planes(planes)
    even = lax.rem(lax.axis_index("gy"), 2) == 0
    for f, ref in enumerate((a_ref, b_ref)):
        for t in range(tiles):
            cols = slice(t * LANES, (t + 1) * LANES)
            for p, out in ((pa, za_ref), (pb, zb_ref)):
                out[f * rows : (f + 1) * rows, cols] = ref[
                    pl.ds(t * planes + p, rows, stride=tiles * planes), :
                ]
            head = ref[t * planes : (t + 1) * planes, :]
            last = (rows - 1) * tiles * planes + t * planes
            tail = ref[last : last + planes, :]
            ya_ref[f * planes : (f + 1) * planes, cols] = jnp.where(even, tail, head)
            yb_ref[f * planes : (f + 1) * planes, cols] = jnp.where(even, head, tail)


def local_kernel(
    dims, a_ref, b_ref, r_ref, s_ref, v_ref, f_ref, rate_ref, c_ref, sh_ref, sl_ref, cells
):
    rows, planes, width = dims
    tiles = width // LANES
    for z in range(planes):
        for t in range(tiles):
            cols = slice(t * LANES, (t + 1) * LANES)
            take = pl.ds(t * planes + z, rows, stride=tiles * planes)
            cells[0, z, :, cols] = a_ref[take, :]
            cells[1, z, :, cols] = b_ref[take, :]
            rate_ref[z, :, cols] = r_ref[take, :]
    row = lax.broadcasted_iota(jnp.int32, (rows, width), 0)
    for z in range(planes):
        react = rate_ref[z] * cells[0, z] * cells[1, z]
        for f, d in enumerate(DIFFUSION):
            c = cells[f, z]
            new = along_x(c, d, v_ref[0])
            north = jnp.where(row == rows - 1, 0.0, pltpu.roll(c, rows - 1, 0))
            south = jnp.where(row == 0, 0.0, pltpu.roll(c, 1, 0))
            new += (d - 0.5 * v_ref[1]) * north + (d + 0.5 * v_ref[1]) * south
            if z < planes - 1:
                new += (d - 0.5 * v_ref[2]) * cells[f, z + 1]
            if z > 0:
                new += (d + 0.5 * v_ref[2]) * cells[f, z - 1]
            f_ref[f, z] = new - react if f == 0 else new + react
    s_high, s_low = split(s_ref[...])
    sh_ref[...] = s_high
    sl_ref[...] = s_low
    edges = jnp.concatenate(
        [cells[0, 0], cells[1, 0], cells[0, planes - 1], cells[1, planes - 1]], axis=0
    )
    c_ref[...] = project(edges, s_high, s_low)


def rows_kernel(dims, f_in, ya_ref, yb_ref, sh_ref, sl_ref, v_ref, f_ref, ea_ref, eb_ref):
    rows, planes, width = dims
    even = lax.rem(lax.axis_index("gy"), 2) == 0
    for f, d in enumerate(DIFFUSION):
        for z in range(planes):
            at = f * planes + z
            first, second = ya_ref[at : at + 1, :], yb_ref[at : at + 1, :]
            north = jnp.where(even, first, second)
            south = jnp.where(even, second, first)
            f_ref[f, z, rows - 1 : rows, :] = (
                f_in[f, z, rows - 1 : rows, :] + (d - 0.5 * v_ref[1]) * north
            )
            f_ref[f, z, 0:1, :] = f_in[f, z, 0:1, :] + (d + 0.5 * v_ref[1]) * south
    pa, pb = edge_planes(planes)
    edges = jnp.concatenate([f_ref[0, pa], f_ref[1, pa], f_ref[0, pb], f_ref[1, pb]], axis=0)
    e = project(edges, sh_ref[...], sl_ref[...])
    ea_ref[...] = e[: 2 * rows]
    eb_ref[...] = e[2 * rows :]


def second_step(a, b, rate, v_ref):
    react = rate * a * b
    return [
        a,
        b,
        along_x(a, DIFFUSION[0], v_ref[0]) - react,
        along_x(b, DIFFUSION[1], v_ref[0]) + react,
    ]


def inner_kernel(dims, f_ref, rate_ref, sh_ref, sl_ref, v_ref, out_ref):
    rows, planes, width = dims
    for z in range(1, planes - 1):
        block = jnp.concatenate(
            second_step(f_ref[0, z], f_ref[1, z], rate_ref[z], v_ref), axis=0
        )
        out = project(block, sh_ref[...], sl_ref[...])
        for i in range(4):
            out_ref[i, z - 1] = out[i * rows : (i + 1) * rows]


def edges_kernel(
    dims, packed, f_ref, rate_ref, za_ref, zb_ref, ea_ref, eb_ref, c_ref, in_ref,
    sh_ref, sl_ref, v_ref, out_ref, p_scr, w_scr,
):
    rows, planes, width = dims
    here, count = lax.axis_index("gz"), lax.axis_size("gz")
    pa, pb = edge_planes(planes)
    blocks = []
    for p, h_ref in ((pa, za_ref), (pb, zb_ref)):
        sign = jnp.where(p == planes - 1, -0.5, 0.5) * v_ref[2]
        a = f_ref[0, p] + (DIFFUSION[0] + sign) * h_ref[:rows, :]
        b = f_ref[1, p] + (DIFFUSION[1] + sign) * h_ref[rows:, :]
        blocks += second_step(a, b, rate_ref[p], v_ref)
    out = project(jnp.concatenate(blocks, axis=0), sh_ref[...], sl_ref[...])
    for f in range(2):
        for z in range(1, planes - 1):
            p_scr[f, z + 1] = in_ref[f, z - 1]
            w_scr[f, z] = in_ref[2 + f, z - 1]
    for i, (p, e_ref) in enumerate(((pa, ea_ref), (pb, eb_ref))):
        upper = p == planes - 1
        step = jnp.where(upper, 1, -1)
        there = here + step
        has = jnp.where(jnp.logical_and(there >= 0, there < count), 1.0, 0.0)
        sign = jnp.where(upper, 0.5, -0.5) * v_ref[2]
        base = pl.multiple_of(jnp.where(upper, 2 * rows, 0), 8)
        for f, d in enumerate(DIFFUSION):
            p_scr[f, p + 1] = out[(4 * i + f) * rows : (4 * i + f + 1) * rows]
            w_scr[f, p] = out[(4 * i + 2 + f) * rows : (4 * i + 3 + f) * rows]
            mine = c_ref[pl.ds(base + f * rows, rows), :]
            p_scr[f, p + 1 + step] = e_ref[f * rows : (f + 1) * rows, :] + (
                has * (d + sign)
            ) * mine
    done = []
    for f, d in enumerate(DIFFUSION):
        for z in range(planes):
            w = (
                w_scr[f, z]
                + (d - 0.5 * v_ref[2]) * p_scr[f, z + 2]
                + (d + 0.5 * v_ref[2]) * p_scr[f, z]
            )
            done.append((w, p_scr[f, z + 1]))
    if not packed:
        for q, pair in enumerate(done):
            out_ref[0, q], out_ref[1, q] = pair
        return
    keep = LANES // packed
    group = lax.broadcasted_iota(jnp.int32, (rows, LANES), 1) // keep
    for i in range(2):
        turned = [pltpu.roll(x[i], q * keep, 1) if q else x[i] for q, x in enumerate(done)]
        for dest in range(packed):
            block = turned[(0 - dest) % packed]
            for g in range(1, packed):
                block = jnp.where(group == g, turned[(g - dest) % packed], block)
            out_ref[dest, i * rows : (i + 1) * rows, :] = block


def sketch_kernel(dims, packed, got_ref, sy_ref, v_ref, out_ref):
    rows, planes, width = dims
    keep = LANES // packed
    total = packed * rows
    w = got_ref[:, :rows, :].reshape(total, LANES)
    p = got_ref[:, rows:, :].reshape(total, LANES)
    row = lax.broadcasted_iota(jnp.int32, (total, LANES), 0)
    north = jnp.where(row == total - 1, 0.0, pltpu.roll(p, total - 1, 0))
    south = jnp.where(row == 0, 0.0, pltpu.roll(p, 1, 0))
    me = lax.axis_index("gy")
    shift = lax.rem((packed - me) * keep, LANES)
    lane = lax.broadcasted_iota(jnp.int32, (total, LANES), 1)
    half = jnp.logical_and(lane >= 0, lane < planes * keep)
    w, north, south = (pltpu.roll(x, shift, 1) for x in (w, north, south))
    d = jnp.where(half, DIFFUSION[0], DIFFUSION[1])
    full = w + (d - 0.5 * v_ref[1]) * north + (d + 0.5 * v_ref[1]) * south
    res = lax.dot_general(
        full.T, sy_ref[...], (((1,), (1,)), ((), ())),
        precision=lax.Precision.HIGHEST, preferred_element_type=F32,
    )
    for q in range(packed):
        out_ref[pl.ds(q, keep, stride=packed), :] = res[q * keep : (q + 1) * keep]


def per_device(fuel, oxidant, rate, velocity, sketch_x, sketch_y):
    dims = rows, planes, width = fuel.shape
    kept = sketch_x.shape[0]
    groups = lax.axis_size("gy")
    count = lax.axis_size("gz")
    mine = kept // groups
    kinds = 2 * planes
    packed = groups if (kept == LANES and mine * kinds == LANES and groups == kinds) else 0
    bind = functools.partial
    a, b, r = lane_view(fuel), lane_view(oxidant), lane_view(rate)

    za, zb, ya, yb = call(
        bind(faces_kernel, dims),
        [((2 * rows, width), F32)] * 2 + [((2 * planes, width), F32)] * 2, 2,
        flops=1 << 20, size=1 << 22,
    )(a, b)
    za = lax.ppermute(za, "gz", swaps(count, 0))
    zb = lax.ppermute(zb, "gz", swaps(count, 1))
    ya = lax.ppermute(ya, "gy", swaps(groups, 0))
    yb = lax.ppermute(yb, "gy", swaps(groups, 1))

    cells = (2, planes, rows, width)
    field, rate_z, own, s_high, s_low = call(
        bind(local_kernel, dims),
        [
            (cells, F32), (cells[1:], F32), ((4 * rows, kept), F32),
            ((kept, width), BF16), ((kept, width), BF16),
        ],
        5, smem=(4,), scratch=[pltpu.VMEM(cells, F32)], flops=1 << 28, size=1 << 23,
    )(a, b, r, sketch_x, velocity)
    field, ea, eb = call(
        bind(rows_kernel, dims),
        [(cells, F32), ((2 * rows, kept), F32), ((2 * rows, kept), F32)],
        6, smem=(5,), aliases={0: 0}, flops=1 << 26, size=1 << 22,
    )(field, ya, yb, s_high, s_low, velocity)
    ea = lax.ppermute(ea, "gz", swaps(count, 0))
    eb = lax.ppermute(eb, "gz", swaps(count, 1))
    (inner,) = call(
        bind(inner_kernel, dims), [((4, planes - 2, rows, kept), F32)],
        5, smem=(4,), flops=1 << 27, size=1 << 22,
    )(field, rate_z, s_high, s_low, velocity)
    shape = (packed, 2 * rows, LANES) if packed else (2, kinds, rows, kept)
    (parts,) = call(
        bind(edges_kernel, dims, packed), [(shape, F32)],
        11, smem=(10,),
        scratch=[
            pltpu.VMEM((2, planes + 2, rows, kept), F32),
            pltpu.VMEM((2, planes, rows, kept), F32),
        ],
        flops=1 << 27, size=1 << 22,
    )(field, rate_z, za, zb, ea, eb, own, inner, s_high, s_low, velocity)
    if packed:
        got = lax.all_to_all(parts, "gy", split_axis=0, concat_axis=0, tiled=True)
        (out,) = call(
            bind(sketch_kernel, dims, packed), [((kept, sketch_y.shape[0]), F32)],
            3, smem=(2,), flops=1 << 24, size=1 << 19,
        )(got, sketch_y, velocity)
        return out.reshape(mine, 2, planes, sketch_y.shape[0])
    got = lax.all_to_all(parts, "gy", split_axis=3, concat_axis=2, tiled=True)
    got = got.reshape(2, 2, planes, groups * rows, mine)
    d = jnp.array(DIFFUSION, F32).reshape(2, 1, 1, 1)
    north = jnp.pad(got[1][:, :, 1:], ((0, 0), (0, 0), (0, 1), (0, 0)))
    south = jnp.pad(got[1][:, :, :-1], ((0, 0), (0, 0), (1, 0), (0, 0)))
    full = got[0] + (d - 0.5 * velocity[1]) * north + (d + 0.5 * velocity[1]) * south
    return jnp.einsum("fzyk,jy->kfzj", full, sketch_y, precision=lax.Precision.HIGHEST)


def solution(mesh):
    in_specs = (P("gy", "gz", None), P("gy", "gz", None), P("gy", "gz", None), P(), P(), P())
    out_specs = P("gy", None, "gz", None)
    return jax.shard_map(
        per_device, mesh=mesh, in_specs=in_specs, out_specs=out_specs, check_vma=False
    )
```
